128 devices in a mesh: row: 16 (over z_hi, y, core), col: 8 (over x, z_lo).
Axes of the slice: x: 4, y: 4, z: 4 (z_hi: 2, z_lo: 2; z = z_hi * 2 + z_lo), core: 2. Of those that a mesh axis runs over, the one named last changes fastest.
Arguments:
- word_topic: bfloat16 [131072, 128], P(('row', 'col')), may hold values from 0.25 to 4
- topic_weight: float32 [128], replicated, may hold values from 0.1 to 10
- tile_blocks: int32 [16, 8, 64, 2], P('row', 'col'), may hold values from 0 to 63, as said below
- tile_live: int32 [16, 8], P('row', 'col'), may hold values from 16 to 64, as said below
- pair_counts: int32 [16, 8, 64, 256, 256], P('row', 'col'), may hold values from 0 to 63
Outputs:
- next_word_topic: bfloat16 [131072, 128], P(('row', 'col'))
- next_topic_weight: float32 [128], replicated
The draws below stay inside these ranges and needn't reach their ends.
Inputs may be any that keep to these rules, and one draw needn't show every extreme that they name: `tile_blocks`: each entry pair is (a word block among the device's 32 blocks of first words, a word block among its 64 blocks of second words); the slots of one device name distinct tiles. `tile_live`: slots at or beyond a device's count hold no tile; some device fills all slots.
All inputs are finite; a program needn't handle non-finite values.
Results may differ from the reference program's by a relative error of at most 0.0049.
Values may be sent and summed in bfloat16 or wider, within the bound.
No kernel may reach another device: no remote copies, remote signals or barrier semaphores. Data moves between devices by JAX's collectives and lax.ppermute only.
A program may use at most 128 MiB of HBM per device.

```python
import math
import jax
import jax.numpy as jnp
from jax import lax

V = 131072
K = 128
BLK = 256
SLOTS = 64
ITERS = 2
SPAN = 1024
ROW_WORDS = 8192
COL_WORDS = 16384
ROW_BLOCKS = 32
COL_BLOCKS = 64
N_ROW = 16
N_COL = 8


def word_groups(key):
    return jax.random.randint(jax.random.fold_in(key, 31), (V,), 0, 8).astype(jnp.int32)


def tile_layout(key):
    devices_all = N_ROW * N_COL
    total = ROW_BLOCKS * COL_BLOCKS
    keys = jax.random.split(jax.random.fold_in(key, 11), devices_all)
    perms = jax.vmap(lambda one_key: jax.random.permutation(one_key, total))(keys)
    chosen = jax.random.randint(jax.random.fold_in(key, 12), (), 0, devices_all)
    picked = perms[chosen]
    where_last = jnp.argmax(picked == total - 1)
    rolled = jnp.roll(picked, -where_last)
    perms = perms.at[chosen].set(rolled)
    tile_ids = perms[:, :SLOTS]
    stacked = jnp.stack([tile_ids // COL_BLOCKS, tile_ids % COL_BLOCKS], axis=-1)
    return stacked.reshape(N_ROW, N_COL, SLOTS, 2).astype(jnp.int32)


def draw_tile_blocks(key, part):
    return tile_layout(key)


def draw_tile_live(key, part):
    devices_all = N_ROW * N_COL
    lowest = max(1, SLOTS // 4)
    counts_all = jax.random.randint(jax.random.fold_in(key, 21), (devices_all,), lowest, SLOTS + 1)
    first_dev = jax.random.randint(jax.random.fold_in(key, 22), (), 0, devices_all)
    other_dev = (first_dev + 1 + jax.random.randint(jax.random.fold_in(key, 23), (), 0, devices_all - 1)) % devices_all
    counts_all = counts_all.at[first_dev].set(SLOTS).at[other_dev].set(lowest)
    return counts_all.reshape(N_ROW, N_COL).astype(jnp.int32)


def draw_word_topic(key, part):
    groups = word_groups(key)
    unit = jax.random.uniform(jax.random.fold_in(key, 32), (V, K), jnp.float32)
    base = 0.25 * jnp.exp(unit * jnp.log(4.0))
    topic_group = jnp.arange(K, dtype=jnp.int32) // (K // 8)
    boost = jnp.where(topic_group[None, :] == groups[:, None], 4.0, 1.0).astype(jnp.float32)
    return (base * boost).astype(jnp.bfloat16)


def draw_pair_counts(key, part):
    groups = word_groups(key)
    blocks = tile_layout(key)
    offsets = jnp.arange(BLK, dtype=jnp.int32)
    col_index = jnp.arange(N_COL, dtype=jnp.int32)

    def one_row(row_pos):
        row_blocks = blocks[row_pos]
        first_local = row_blocks[:, :, 0][:, :, None] * BLK + offsets
        first_word = row_pos * ROW_WORDS + first_local
        second_local = row_blocks[:, :, 1][:, :, None] * BLK + offsets
        second_word = (second_local // SPAN * N_COL + col_index[:, None, None]) * SPAN + second_local % SPAN
        first_group = groups[first_word]
        second_group = groups[second_word]
        same = first_group[:, :, :, None] == second_group[:, :, None, :]
        raw = jax.random.randint(jax.random.fold_in(jax.random.fold_in(key, 41), row_pos), (N_COL, SLOTS, BLK, BLK), 0, 64)
        return jnp.where(same, raw, raw % 3).astype(jnp.int32)
    return lax.map(one_row, jnp.arange(N_ROW, dtype=jnp.int32))


def setup_inputs(seed: int = 0) -> dict:
    splits = jax.random.split(jax.random.key(seed), 6)
    word_topic = draw_word_topic(jax.random.fold_in(splits[5], 71), 0)
    topic_weight = jnp.clip(jnp.exp(jax.random.uniform(splits[1], (K,), jnp.float32, math.log(0.1), math.log(10.0))), 0.1, 10.0)
    tile_blocks = draw_tile_blocks(jax.random.fold_in(splits[5], 71), 0)
    tile_live = draw_tile_live(jax.random.fold_in(splits[5], 71), 0)
    pair_counts = draw_pair_counts(jax.random.fold_in(splits[5], 71), 0)
    return {"word_topic": word_topic, "topic_weight": topic_weight, "tile_blocks": tile_blocks, "tile_live": tile_live, "pair_counts": pair_counts}


def tile_terms(scaled, col_phi, blocks, live, tiles_all):
    left_blocks = scaled.reshape(-1, BLK, K)
    right_blocks = col_phi.reshape(-1, BLK, K)
    tile_group = 8

    def group_step(group, carry):
        row_acc, col_acc = carry
        start = (group * tile_group).astype(jnp.int32)
        row_ids = lax.dynamic_slice_in_dim(blocks[:, 0], start, tile_group)
        col_ids = lax.dynamic_slice_in_dim(blocks[:, 1], start, tile_group)
        tiles = lax.dynamic_slice_in_dim(tiles_all, start, tile_group, 0)
        alive = (start + jnp.arange(tile_group, dtype=jnp.int32)) < live
        left = left_blocks[row_ids].astype(jnp.float32)
        right = right_blocks[col_ids].astype(jnp.float32)
        denoms = jnp.einsum("gak,gbk->gab", left, right)
        ratio = jnp.where(alive[:, None, None], tiles.astype(jnp.float32) / denoms, 0.0).astype(jnp.bfloat16)
        ratio_wide = ratio.astype(jnp.float32)
        row_part = jnp.einsum("gab,gbk->gak", ratio_wide, right)
        col_part = jnp.einsum("gab,gak->gbk", ratio_wide, left)
        return row_acc.at[row_ids].add(row_part), col_acc.at[col_ids].add(col_part)

    start_row = jnp.zeros(left_blocks.shape, jnp.float32)
    start_col = jnp.zeros(right_blocks.shape, jnp.float32)
    turns = (live + tile_group - 1) // tile_group
    row_acc, col_acc = lax.fori_loop(0, turns, group_step, (start_row, start_col))
    return row_acc.reshape(-1, K), col_acc.reshape(-1, K)


def reference(word_topic, topic_weight, tile_blocks, tile_live, pair_counts):
    weights = word_topic
    shares = topic_weight
    for step in range(ITERS):
        grid_phi = weights.reshape(N_ROW, N_COL, SPAN, K)

        def device_step(index, carry):
            row_total, col_total = carry
            index = jnp.asarray(index).astype(jnp.int32)
            rpos = index // N_COL
            cpos = index % N_COL
            row_phi = grid_phi[rpos].reshape(ROW_WORDS, K)
            col_phi = grid_phi[:, cpos].reshape(COL_WORDS, K)
            scaled = (row_phi.astype(jnp.float32) * shares).astype(jnp.bfloat16)
            row_terms, col_terms = tile_terms(scaled, col_phi, tile_blocks[rpos, cpos], tile_live[rpos, cpos], pair_counts[rpos, cpos])
            row_total = row_total.at[rpos].add(row_terms.reshape(N_COL, SPAN, K))
            col_total = col_total.at[:, cpos].add(col_terms.reshape(N_ROW, SPAN, K))
            return row_total, col_total

        zero_grid = jnp.zeros((N_ROW, N_COL, SPAN, K), jnp.float32)
        row_total, col_total = lax.fori_loop(0, N_ROW * N_COL, device_step, (zero_grid, zero_grid))
        expected = (grid_phi.astype(jnp.float32) * (shares * row_total + col_total)).reshape(V, K)
        totals = jnp.sum(expected, axis=0)
        weights = (V * expected / totals).astype(jnp.bfloat16)
        shares = K * totals / jnp.sum(totals)
    return weights, shares
```

```python
import jax
import jax.numpy as jnp
from jax import lax
from jax.experimental import pallas as pl
from jax.experimental.pallas import tpu as pltpu
from jax.sharding import PartitionSpec as P

V = 131072
K = 128
BLK = 256
SLOTS = 64
ITERS = 2
SPAN = 1024
GROUP = 8
AXES = ("row", "col")
ROW_PARTS = (("zh", 2), ("y", 4), ("k", 2))
COL_PARTS = (("x", 4), ("zl", 2))
SIZES = dict(ROW_PARTS + COL_PARTS)


def parts_of(index):
    out = {}
    for name, size in reversed(ROW_PARTS + COL_PARTS):
        out[name] = index % size
        index = index // size
    return out


def index_of(parts):
    index = 0
    for name, size in ROW_PARTS + COL_PARTS:
        index = index * size + parts[name]
    return index


def send(value, part, step):
    pairs = []
    for source in range(128):
        target = parts_of(source)
        target[part] = (target[part] + step) % SIZES[part]
        pairs.append((source, index_of(target)))
    return lax.ppermute(value, AXES, pairs)


def coords():
    row, col = lax.axis_index("row"), lax.axis_index("col")
    return {"zh": row // 8, "y": (row // 2) % 4, "k": row % 2, "x": col // 2, "zl": col % 2}


def tiles_kernel(
    blocks, live, pos, shares, r0, r1, r2, r3, c00, c01, c02, c03, c10, c11, c12, c13, tiles,
    x0, x1, x2, x3, k0, k1, k2, k3, s0, s1, s2, s3, totals,
    rows, scaled, cols, row_acc, col_acc, sem,
):
    group = pl.program_id(0)
    zh, y, k, x, zl = pos[0], pos[1], pos[2], pos[3], pos[4]

    def row_span(back, other):
        return (x + 4 - back) % 4 * 2 + (zl + other) % 2

    def col_span(other_k, back, other):
        return ((zh + other) % 2 * 4 + (y + 4 - back) % 4) * 2 + (k + other_k) % 2

    def at(span):
        return pl.ds(pl.multiple_of(span * SPAN, SPAN), SPAN)

    @pl.when(group == 0)
    def _():
        copies = []
        for back, ref in enumerate((r0, r1, r2, r3)):
            for other in range(2):
                half = ref.at[pl.ds(other * SPAN, SPAN), :]
                copies.append((half, rows.at[at(row_span(back, other)), :]))
        for other_k, refs in enumerate(((c00, c01, c02, c03), (c10, c11, c12, c13))):
            for back, ref in enumerate(refs):
                for other in range(2):
                    half = ref.at[pl.ds(other * SPAN, SPAN), :]
                    copies.append((half, cols.at[at(col_span(other_k, back, other)), :]))
        started = [
            pltpu.make_async_copy(source, target, sem.at[i])
            for i, (source, target) in enumerate(copies)
        ]
        for copy in started:
            copy.start()
        row_acc[...] = jnp.zeros_like(row_acc)
        col_acc[...] = jnp.zeros_like(col_acc)
        for copy in started:
            copy.wait()
        scaled[...] = (rows[...].astype(jnp.float32) * shares[...]).astype(jnp.bfloat16)

    alive = live[0]

    @pl.when(group * GROUP < alive)
    def _():
        for t in range(GROUP):
            slot = group * GROUP + t
            p = pl.multiple_of(jnp.clip(blocks[2 * slot], 0, 31) * BLK, BLK)
            q = pl.multiple_of(jnp.clip(blocks[2 * slot + 1], 0, 63) * BLK, BLK)
            left = scaled[pl.ds(p, BLK), :]
            right = cols[pl.ds(q, BLK), :]
            denom = lax.dot_general(
                left, right, (((1,), (1,)), ((), ())), preferred_element_type=jnp.float32
            )
            ratio = jnp.where(slot < alive, tiles[t].astype(jnp.float32) / denom, 0.0)
            ratio = ratio.astype(jnp.bfloat16)
            row_acc[pl.ds(p, BLK), :] += jnp.dot(ratio, right, preferred_element_type=jnp.float32)
            col_acc[pl.ds(q, BLK), :] += lax.dot_general(
                ratio, left, (((0,), (0,)), ((), ())), preferred_element_type=jnp.float32
            )

    @pl.when(group == pl.num_programs(0) - 1)
    def _():
        total = jnp.zeros((8, K), jnp.float32)
        for step, ref in enumerate((x0, x1, x2, x3)):
            for other in range(2):
                span = (x + step) % 4 * 2 + (zl + other) % 2
                terms = row_acc[at(span), :]
                both = terms * (rows[at(span), :].astype(jnp.float32) * shares[...])
                total += jnp.sum(both.reshape(SPAN // 8, 8, K), axis=0)
                ref[pl.ds(other * SPAN, SPAN), :] = terms.astype(ref.dtype)
        for other_k, refs in enumerate(((k0, k1, k2, k3), (s0, s1, s2, s3))):
            for step, ref in enumerate(refs):
                for other in range(2):
                    span = ((zh + other) % 2 * 4 + (y + step) % 4) * 2 + (k + other_k) % 2
                    terms = col_acc[at(span), :]
                    both = terms * cols[at(span), :].astype(jnp.float32)
                    total += jnp.sum(both.reshape(SPAN // 8, 8, K), axis=0)
                    ref[pl.ds(other * SPAN, SPAN), :] = terms.astype(ref.dtype)
        totals[...] = jnp.broadcast_to(jnp.sum(total, axis=0, keepdims=True), (8, K))


def sweep(blocks, live, pos, shares, row_parts, col_parts, tiles):
    whole = pl.BlockSpec(memory_space=pl.ANY)
    kept = pl.BlockSpec((2 * SPAN, K), lambda g, *_: (0, 0))

    def tile_at(g, blocks, live, pos):
        return (jnp.minimum(g, (live[0] - 1) // GROUP), 0, 0)

    f32 = jax.ShapeDtypeStruct((2 * SPAN, K), jnp.float32)
    b16 = jax.ShapeDtypeStruct((2 * SPAN, K), jnp.bfloat16)
    return pl.pallas_call(
        tiles_kernel,
        grid_spec=pltpu.PrefetchScalarGridSpec(
            num_scalar_prefetch=3,
            grid=(SLOTS // GROUP,),
            in_specs=[pl.BlockSpec((1, K), lambda g, *_: (0, 0))]
            + [whole] * 12
            + [pl.BlockSpec((GROUP, BLK, BLK), tile_at)],
            out_specs=[kept] * 12 + [pl.BlockSpec((8, K), lambda g, *_: (0, 0))],
            scratch_shapes=[
                pltpu.VMEM((8 * SPAN, K), jnp.bfloat16),
                pltpu.VMEM((8 * SPAN, K), jnp.bfloat16),
                pltpu.VMEM((16 * SPAN, K), jnp.bfloat16),
                pltpu.VMEM((8 * SPAN, K), jnp.float32),
                pltpu.VMEM((16 * SPAN, K), jnp.float32),
                pltpu.SemaphoreType.DMA((24,)),
            ],
        ),
        out_shape=[f32, b16, b16, b16]
        + [f32] * 4
        + [b16] * 4
        + [jax.ShapeDtypeStruct((8, K), jnp.float32)],
        compiler_params=pltpu.CompilerParams(vmem_limit_bytes=58 << 20),
        name="tiles",
    )(blocks, live, pos, shares.reshape(1, K), *row_parts, *col_parts, tiles)


def gather_words(weights):
    with jax.named_scope("gather_z"):
        low = send(weights, "zl", 1)
        high = send(weights, "zh", 1)
    row_own = jnp.concatenate([weights, low])
    col_own = jnp.concatenate([weights, high])
    with jax.named_scope("gather_xy"):
        col_parts = [col_own] + [send(col_own, "y", s) for s in (1, 2, 3)]
        row_parts = [row_own] + [send(row_own, "x", s) for s in (1, 2, 3)]
    with jax.named_scope("gather_core"):
        col_other = [send(part, "k", 1) for part in col_parts]
    return row_parts, col_parts + col_other


def sum_everywhere(value, at):
    value = value + send(value, "k", 1)
    for part in ("x", "y"):
        stack = jnp.stack([value] + [send(value, part, s) for s in (3, 2, 1)])
        value = jnp.sum(jnp.roll(stack, at[part], axis=0), axis=0)
    value = value + send(value, "zl", 1)
    return value + send(value, "zh", 1)


def local(word_topic, topic_weight, tile_blocks, tile_live, pair_counts):
    at = coords()
    pos = jnp.stack([at[n] for n in ("zh", "y", "k", "x", "zl")]).astype(jnp.int32)
    blocks = tile_blocks.reshape(2 * SLOTS)
    live = tile_live.reshape(1)
    tiles = pair_counts.reshape(SLOTS, BLK, BLK)
    weights = word_topic
    shares = topic_weight
    for _ in range(ITERS):
        row_parts, col_parts = gather_words(weights)
        outs = sweep(blocks, live, pos, shares, row_parts, col_parts, tiles)
        x_kept, x_sent = outs[0], outs[1:4]
        k_kept, k_sent = outs[4:8], outs[8:12]
        totals = sum_everywhere(outs[12], at)[0]
        with jax.named_scope("scatter_core"):
            k_got = {s: send(k_sent[s], "k", 1) for s in (1, 2, 3, 0)}
        with jax.named_scope("scatter_x"):
            x_got = [send(x_sent[s - 1], "x", s).astype(jnp.float32) for s in (1, 2, 3)]
        y_sum = {s: k_kept[s] + k_got[s].astype(jnp.float32) for s in (1, 2, 3, 0)}
        with jax.named_scope("scatter_y"):
            y_got = [
                send(y_sum[s].astype(jnp.bfloat16), "y", s).astype(jnp.float32) for s in (1, 2, 3)
            ]
        x_sum = x_kept + x_got[0] + x_got[1] + x_got[2]
        y_all = y_sum[0] + y_got[0] + y_got[1] + y_got[2]
        with jax.named_scope("scatter_z"):
            low = send(x_sum[SPAN:].astype(jnp.bfloat16), "zl", 1)
            high = send(y_all[SPAN:].astype(jnp.bfloat16), "zh", 1)
        row_sum = x_sum[:SPAN] + low.astype(jnp.float32)
        col_sum = y_all[:SPAN] + high.astype(jnp.float32)
        expected = weights.astype(jnp.float32) * (shares * row_sum + col_sum)
        weights = (V * expected / totals).astype(jnp.bfloat16)
        shares = K * totals / jnp.sum(totals)
    return (weights, shares)


def solution(mesh):
    in_specs = (
        P(("row", "col"), None),
        P(),
        P("row", "col", None, None),
        P("row", "col"),
        P("row", "col", None, None, None),
    )
    out_specs = (P(("row", "col"), None), P())
    return jax.shard_map(local, mesh=mesh, in_specs=in_specs, out_specs=out_specs, check_vma=False)
```

```python
from functools import partial

import jax
import jax.numpy as jnp
from jax import lax
from jax.experimental import pallas as pl
from jax.experimental.pallas import tpu as pltpu
from jax.sharding import PartitionSpec as P

V = 131072
K = 128
BLK = 256
SLOTS = 64
ITERS = 2
SPAN = 1024
GROUP = 8
EXTRA = 16
VMEM_MIB = 44
AXES = ("row", "col")
ROW_PARTS = (("zh", 2), ("y", 4), ("k", 2))
COL_PARTS = (("x", 4), ("zl", 2))
SIZES = dict(ROW_PARTS + COL_PARTS)


def parts_of(index):
    out = {}
    for name, size in reversed(ROW_PARTS + COL_PARTS):
        out[name] = index % size
        index = index // size
    return out


def index_of(parts):
    index = 0
    for name, size in ROW_PARTS + COL_PARTS:
        index = index * size + parts[name]
    return index


def send(value, part, step):
    pairs = []
    for source in range(128):
        target = parts_of(source)
        target[part] = (target[part] + step) % SIZES[part]
        pairs.append((source, index_of(target)))
    return lax.ppermute(value, AXES, pairs)


def together(*parts):
    groups = {}
    for place in range(128):
        key = parts_of(place)
        for part in parts:
            key.pop(part)
        groups.setdefault(tuple(key.values()), []).append(place)
    return list(groups.values())


def coords():
    row, col = lax.axis_index("row"), lax.axis_index("col")
    return {"zh": row // 8, "y": (row // 2) % 4, "k": row % 2, "x": col // 2, "zl": col % 2}


def placed(tile_blocks, at):
    p = jnp.clip(tile_blocks[:, 0], 0, 31)
    q = jnp.clip(tile_blocks[:, 1], 0, 63)
    row_span, col_span = p // 4, q // 4
    row_at = (at["x"] + 4 - row_span // 2) % 4 * 2 + (row_span + at["zl"]) % 2
    col_at = (col_span + at["k"]) % 2 * 8 + col_span // 2
    return jnp.concatenate([row_at * 4 + p % 4, col_at * 4 + q % 4]).astype(jnp.int32)


def in_parts(value):
    high = lax.reduce_precision(value, 8, 7)
    middle = lax.reduce_precision(value - high, 8, 7)
    low = value - high - middle
    rows = jnp.stack([high, middle, low])
    return jnp.pad(rows, ((0, EXTRA - 3), (0, 0))).astype(jnp.bfloat16)


def joined(rows):
    rows = rows.astype(jnp.float32)
    return rows[0] + rows[1] + rows[2]


def tiles_kernel(
    first, places, live, shares_in, row_0, row_1, row_2, row_3, own_in, other_in, tiles_in,
    x_0, x_1, x_2, x_3, k_hbm, s_hbm, rows, scaled, cols, shared, tiles, ratios, row_acc, col_acc,
    x_out, k_out, s_out, sem, tile_sem, out_sem,
):
    f32, b16 = jnp.float32, jnp.bfloat16
    row_in = (row_0, row_1, row_2, row_3)
    copies = []
    for i in range(4):
        source = row_in[i].at[pl.ds(0, 2 * SPAN), :]
        copies.append((source, rows.at[pl.ds(2 * i * SPAN, 2 * SPAN), :]))
    if not first:
        for i in range(4):
            source = row_in[i].at[pl.ds(2 * SPAN, EXTRA), :]
            copies.append((source, shared.at[pl.ds(i * EXTRA, EXTRA), :]))
    row_copies = len(copies)
    copies.append((own_in, cols.at[pl.ds(0, 8 * SPAN), :]))
    copies.append((other_in, cols.at[pl.ds(8 * SPAN, 8 * SPAN), :]))
    started = [
        pltpu.make_async_copy(source, target, sem.at[i])
        for i, (source, target) in enumerate(copies)
    ]
    for copy in started:
        copy.start()
    alive = live[0]
    turns = (alive + GROUP - 1) // GROUP

    def fetch(group):
        span = pl.ds(group * GROUP, GROUP)
        return pltpu.make_async_copy(tiles_in.at[span], tiles.at[span], tile_sem.at[group])

    def start(group, carry):
        fetch(group).start()
        return carry

    lax.fori_loop(0, turns, start, 0)
    row_acc[...] = jnp.zeros_like(row_acc)
    col_acc[...] = jnp.zeros_like(col_acc)
    for copy in started[:row_copies]:
        copy.wait()
    if first:
        shares = shares_in[...]
    else:
        totals = jnp.sum(shared[...].astype(f32), axis=0, keepdims=True)
        shares = (K * V / jnp.sum(totals)) * (V / totals)
    scaled[...] = (rows[...].astype(f32) * shares).astype(b16)
    for copy in started[row_copies:]:
        copy.wait()

    def group_step(group, carry):
        fetch(group).wait()
        where = []
        for t in range(GROUP):
            slot = group * GROUP + t
            p = pl.ds(pl.multiple_of(places[slot] * BLK, BLK), BLK)
            q = pl.ds(pl.multiple_of(places[SLOTS + slot] * BLK, BLK), BLK)
            where.append((p, q))
            denom = lax.dot_general(
                scaled[p, :], cols[q, :], (((1,), (1,)), ((), ())), preferred_element_type=f32
            )
            ratio = jnp.where(slot < alive, tiles[slot].astype(f32) / denom, 0.0)
            ratios[t] = ratio.astype(b16)
        for t, (p, q) in enumerate(where):
            row_acc[p, :] += jnp.dot(ratios[t], cols[q, :], preferred_element_type=f32)
            col_acc[q, :] += lax.dot_general(
                ratios[t], scaled[p, :], (((0,), (0,)), ((), ())), preferred_element_type=f32
            )
        return carry

    lax.fori_loop(0, turns, group_step, 0)

    total = jnp.zeros((8, K), f32)
    for i in range(8):
        span = pl.ds(i * SPAN, SPAN)
        terms = row_acc[span, :]
        both = terms * (rows[span, :].astype(f32) * shares + scaled[span, :].astype(f32))
        total += jnp.sum(both.reshape(SPAN // 8, 8, K), axis=0)
        x_out[span, :] = terms.astype(b16)
    written = []
    for step, ref in enumerate((x_0, x_1, x_2, x_3)):
        source = x_out.at[pl.ds((4 - step) % 4 * 2 * SPAN, 2 * SPAN), :]
        written.append(pltpu.make_async_copy(source, ref, out_sem.at[2 + step]))
        written[-1].start()
    total = jnp.sum(total, axis=0, keepdims=True)
    high = total.astype(b16).astype(f32)
    middle = (total - high).astype(b16).astype(f32)
    low = total - high - middle
    at = lax.broadcasted_iota(jnp.int32, (EXTRA, K), 0)
    zero = jnp.zeros((EXTRA, K), f32)
    out = jnp.where(at == 0, high, jnp.where(at == 1, middle, jnp.where(at == 2, low, zero)))
    for i, (ref, hbm) in enumerate(((s_out, s_hbm), (k_out, k_hbm))):
        ref[pl.ds(8 * SPAN, EXTRA), :] = out.astype(b16)
        ref[pl.ds(0, 8 * SPAN), :] = col_acc[pl.ds((1 - i) * 8 * SPAN, 8 * SPAN), :].astype(b16)
        written.append(pltpu.make_async_copy(ref, hbm, out_sem.at[i]))
        written[-1].start()
    for copy in written:
        copy.wait()


def sweep(first, places, live, shares, rows, own_in, other_in, tiles):
    whole = pl.BlockSpec(memory_space=pl.ANY)
    near = pl.BlockSpec(memory_space=pltpu.VMEM)
    far = pl.BlockSpec(memory_space=pltpu.HBM)
    scalars = pl.BlockSpec(memory_space=pltpu.SMEM)
    return pl.pallas_call(
        partial(tiles_kernel, first),
        in_specs=[scalars, scalars, near] + [whole] * 6 + [far],
        out_specs=[far] * 6,
        scratch_shapes=[
            pltpu.VMEM((8 * SPAN, K), jnp.bfloat16),
            pltpu.VMEM((8 * SPAN, K), jnp.bfloat16),
            pltpu.VMEM((16 * SPAN, K), jnp.bfloat16),
            pltpu.VMEM((4 * EXTRA, K), jnp.bfloat16),
            pltpu.VMEM((SLOTS, BLK, BLK), jnp.bfloat16),
            pltpu.VMEM((GROUP, BLK, BLK), jnp.bfloat16),
            pltpu.VMEM((8 * SPAN, K), jnp.float32),
            pltpu.VMEM((16 * SPAN, K), jnp.float32),
            pltpu.VMEM((8 * SPAN, K), jnp.bfloat16),
            pltpu.VMEM((8 * SPAN + EXTRA, K), jnp.bfloat16),
            pltpu.VMEM((8 * SPAN + EXTRA, K), jnp.bfloat16),
            pltpu.SemaphoreType.DMA((10,)),
            pltpu.SemaphoreType.DMA((SLOTS // GROUP,)),
            pltpu.SemaphoreType.DMA((6,)),
        ],
        out_shape=[jax.ShapeDtypeStruct((2 * SPAN, K), jnp.bfloat16)] * 4
        + [
            jax.ShapeDtypeStruct((8 * SPAN + EXTRA, K), jnp.bfloat16),
            jax.ShapeDtypeStruct((8 * SPAN + EXTRA, K), jnp.bfloat16),
        ],
        compiler_params=pltpu.CompilerParams(vmem_limit_bytes=VMEM_MIB << 20),
        name="tiles",
    )(places, live, shares.reshape(1, K), *rows, own_in, other_in, tiles)


def after(value, *others):
    return lax.optimization_barrier((value, *others))[0]


def gather_words(weights, totals, tiles):
    if totals is None:
        low = send(weights, "zl", 1)
        row_sent = jnp.concatenate([weights, low])
    else:
        low = send(jnp.concatenate([weights, in_parts(totals)]), "zl", 1)
        both = in_parts(totals + joined(low[SPAN:]))
        row_sent = jnp.concatenate([weights, low[:SPAN], both])
    rows = [row_sent] + [send(row_sent, "x", s) for s in (1, 2, 3)]
    copies = after(jnp.broadcast_to(weights[None], (8, SPAN, K)), row_sent)
    own = lax.all_to_all(copies, AXES, 0, 0, axis_index_groups=together("zh", "y"))
    if totals is None:
        tiles = after(tiles, row_sent).astype(jnp.bfloat16)
        own = after(own, tiles)
    own = after(own, *rows[1:])
    own = own.reshape(8 * SPAN, K)
    return (rows, own, send(own, "k", 1)), tiles


def scatter_terms(x_0, x_1, x_2, x_3, k_out, s_out):
    f32, b16 = jnp.float32, jnp.bfloat16
    x_got = [send(x, "x", s + 1) for s, x in enumerate((x_1, x_2, x_3))]
    x_sum = x_0.astype(f32) + sum(x.astype(f32) for x in x_got)
    s_got = send(s_out, "k", 1)
    both = k_out[: 8 * SPAN].astype(f32) + s_got[: 8 * SPAN].astype(f32)
    pair = in_parts(joined(k_out[8 * SPAN :]) + joined(s_got[8 * SPAN :]))
    sent = jnp.concatenate(
        [both.astype(b16).reshape(8, SPAN, K), jnp.broadcast_to(pair[None], (8, EXTRA, K))], axis=1
    )
    got = lax.all_to_all(sent, AXES, 0, 0, axis_index_groups=together("zh", "y"))
    low = send(x_sum[SPAN:].astype(b16), "zl", 1)
    got = after(got, low)
    col_sum = jnp.sum(got[:, :SPAN].astype(f32), axis=0)
    totals = jnp.sum(got[:, SPAN:].astype(f32), axis=(0, 1))
    row_sum = x_sum[:SPAN] + low.astype(f32)
    return row_sum, col_sum, totals


def sum_columns(value, at):
    value = jnp.broadcast_to(value[None], (8, K))
    stack = jnp.stack([value] + [send(value, "x", s) for s in (3, 2, 1)])
    value = jnp.sum(jnp.roll(stack, at["x"], axis=0), axis=0)
    return (value + send(value, "zl", 1))[0]


def local(word_topic, topic_weight, tile_blocks, tile_live, pair_counts):
    at = coords()
    places = placed(tile_blocks[0, 0], at)
    live = tile_live.reshape(1)
    tiles = pair_counts.reshape(SLOTS, BLK, BLK)
    weights, shares, totals = word_topic, topic_weight, None
    for step in range(ITERS):
        gathered, tiles = gather_words(weights, totals, tiles)
        outs = sweep(step == 0, places, live, shares, *gathered, tiles)
        row_sum, col_sum, totals = scatter_terms(*outs)
        if step > 0:
            shares = (K * V / jnp.sum(before)) * (V / before)
        expected = weights.astype(jnp.float32) * (shares * row_sum + col_sum)
        if step < ITERS - 1:
            weights = expected.astype(jnp.bfloat16)
            before = sum_columns(totals, at)
    totals = sum_columns(totals, at)
    return (V * expected / totals).astype(jnp.bfloat16), K * totals / jnp.sum(totals)


def solution(mesh):
    in_specs = (
        P(("row", "col"), None),
        P(),
        P("row", "col", None, None),
        P("row", "col"),
        P("row", "col", None, None, None),
    )
    out_specs = (P(("row", "col"), None), P())
    return jax.shard_map(local, mesh=mesh, in_specs=in_specs, out_specs=out_specs, check_vma=False)
```

```python
from functools import partial

import jax
import jax.numpy as jnp
from jax import lax
from jax.experimental import pallas as pl
from jax.experimental.pallas import tpu as pltpu
from jax.sharding import PartitionSpec as P

V = 131072
K = 128
BLK = 256
SLOTS = 64
ITERS = 2
SPAN = 1024
GROUP = 8
EXTRA = 16
VMEM_MIB = 44
AXES = ("row", "col")
ROW_PARTS = (("zh", 2), ("y", 4), ("k", 2))
COL_PARTS = (("x", 4), ("zl", 2))
SIZES = dict(ROW_PARTS + COL_PARTS)


def parts_of(index):
    out = {}
    for name, size in reversed(ROW_PARTS + COL_PARTS):
        out[name] = index % size
        index = index // size
    return out


def index_of(parts):
    index = 0
    for name, size in ROW_PARTS + COL_PARTS:
        index = index * size + parts[name]
    return index


def send(value, part, step):
    pairs = []
    for source in range(128):
        target = parts_of(source)
        target[part] = (target[part] + step) % SIZES[part]
        pairs.append((source, index_of(target)))
    return lax.ppermute(value, AXES, pairs)


def together(*parts):
    groups = {}
    for place in range(128):
        key = parts_of(place)
        for part in parts:
            key.pop(part)
        groups.setdefault(tuple(key.values()), []).append(place)
    return list(groups.values())


def coords():
    row, col = lax.axis_index("row"), lax.axis_index("col")
    return {"zh": row // 8, "y": (row // 2) % 4, "k": row % 2, "x": col // 2, "zl": col % 2}


def placed(tile_blocks, at):
    p = jnp.clip(tile_blocks[:, 0], 0, 31)
    q = jnp.clip(tile_blocks[:, 1], 0, 63)
    row_span, col_span = p // 4, q // 4
    row_at = (at["x"] + 4 - row_span // 2) % 4 * 2 + (row_span + at["zl"]) % 2
    col_at = (col_span + at["k"]) % 2 * 8 + col_span // 2
    return jnp.concatenate([row_at * 4 + p % 4, col_at * 4 + q % 4]).astype(jnp.int32)


def in_parts(value):
    high = lax.reduce_precision(value, 8, 7)
    middle = lax.reduce_precision(value - high, 8, 7)
    low = value - high - middle
    rows = jnp.stack([high, middle, low])
    return jnp.pad(rows, ((0, EXTRA - 3), (0, 0))).astype(jnp.bfloat16)


def joined(rows):
    rows = rows.astype(jnp.float32)
    return rows[0] + rows[1] + rows[2]


def tiles_kernel(
    first, places, live, shares_in, row_0, row_1, row_2, row_3, own_in, other_in, tiles_in,
    x_00, x_01, x_10, x_11, x_20, x_21, x_30, x_31, k_hbm, s_hbm, shares_out,
    rows, scaled, cols, shared, tiles, ratios, row_acc, col_acc,
    x_out, k_out, s_out, sem, tile_sem, out_sem,
):
    f32, b16 = jnp.float32, jnp.bfloat16
    row_in = (row_0, row_1, row_2, row_3)
    copies = []
    for i in range(4):
        source = row_in[i].at[pl.ds(0, 2 * SPAN), :]
        copies.append((source, rows.at[pl.ds(2 * i * SPAN, 2 * SPAN), :]))
    if not first:
        for i in range(4):
            source = row_in[i].at[pl.ds(2 * SPAN, EXTRA), :]
            copies.append((source, shared.at[pl.ds(i * EXTRA, EXTRA), :]))
    row_copies = len(copies)
    copies.append((own_in, cols.at[pl.ds(0, 8 * SPAN), :]))
    copies.append((other_in, cols.at[pl.ds(8 * SPAN, 8 * SPAN), :]))
    started = [
        pltpu.make_async_copy(source, target, sem.at[i])
        for i, (source, target) in enumerate(copies)
    ]
    for copy in started:
        copy.start()
    alive = live[0]
    turns = (alive + GROUP - 1) // GROUP

    def fetch(group):
        span = pl.ds(group * GROUP, GROUP)
        return pltpu.make_async_copy(tiles_in.at[span], tiles.at[span], tile_sem.at[group])

    def start(group, carry):
        fetch(group).start()
        return carry

    lax.fori_loop(0, turns, start, 0)
    row_acc[...] = jnp.zeros_like(row_acc)
    col_acc[...] = jnp.zeros_like(col_acc)
    for copy in started[:row_copies]:
        copy.wait()
    if first:
        shares = shares_in[...]
    else:
        totals = jnp.sum(shared[...].astype(f32), axis=0, keepdims=True)
        shares = (K * V / jnp.sum(totals)) * (V / totals)
    shares_out[...] = jnp.broadcast_to(shares, (8, K))
    scaled[...] = (rows[...].astype(f32) * shares).astype(b16)
    for copy in started[row_copies:]:
        copy.wait()

    def group_step(group, carry):
        fetch(group).wait()
        where = []
        for t in range(GROUP):
            slot = group * GROUP + t
            p = pl.ds(pl.multiple_of(places[slot] * BLK, BLK), BLK)
            q = pl.ds(pl.multiple_of(places[SLOTS + slot] * BLK, BLK), BLK)
            where.append((p, q))
            denom = lax.dot_general(
                scaled[p, :], cols[q, :], (((1,), (1,)), ((), ())), preferred_element_type=f32
            )
            ratio = jnp.where(slot < alive, tiles[slot].astype(f32) / denom, 0.0)
            ratios[t] = ratio.astype(b16)
        for t, (p, q) in enumerate(where):
            row_acc[p, :] += jnp.dot(ratios[t], cols[q, :], preferred_element_type=f32)
            col_acc[q, :] += lax.dot_general(
                ratios[t], scaled[p, :], (((0,), (0,)), ((), ())), preferred_element_type=f32
            )
        return carry

    lax.fori_loop(0, turns, group_step, 0)

    total = jnp.zeros((8, K), f32)
    for i in range(8):
        span = pl.ds(i * SPAN, SPAN)
        terms = row_acc[span, :]
        both = terms * (rows[span, :].astype(f32) * shares + scaled[span, :].astype(f32))
        total += jnp.sum(both.reshape(SPAN // 8, 8, K), axis=0)
        x_out[span, :] = terms.astype(b16)
    written = []
    for i, ref in enumerate((x_00, x_01, x_10, x_11, x_20, x_21, x_30, x_31)):
        source = x_out.at[pl.ds(((4 - i // 2) % 4 * 2 + i % 2) * SPAN, SPAN), :]
        written.append(pltpu.make_async_copy(source, ref, out_sem.at[2 + i]))
        written[-1].start()
    total = jnp.sum(total, axis=0, keepdims=True)
    high = total.astype(b16).astype(f32)
    middle = (total - high).astype(b16).astype(f32)
    low = total - high - middle
    at = lax.broadcasted_iota(jnp.int32, (EXTRA, K), 0) - 3
    zero = jnp.zeros((EXTRA, K), f32)
    for i, (ref, hbm) in enumerate(((s_out, s_hbm), (k_out, k_hbm))):
        at = at + 3 * i
        out = jnp.where(at == 0, high, jnp.where(at == 1, middle, jnp.where(at == 2, low, zero)))
        for j in range(8):
            source = pl.ds(((1 - i) * 8 + j) * SPAN, SPAN)
            ref[pl.ds(j * (SPAN + EXTRA), SPAN), :] = col_acc[source, :].astype(b16)
            ref[pl.ds(j * (SPAN + EXTRA) + SPAN, EXTRA), :] = out.astype(b16)
        written.append(pltpu.make_async_copy(ref, hbm, out_sem.at[i]))
        written[-1].start()
    for copy in written:
        copy.wait()


def sweep(first, places, live, shares, rows, own_in, other_in, tiles):
    near = pl.BlockSpec(memory_space=pltpu.VMEM)
    far = pl.BlockSpec(memory_space=pl.ANY)
    scalars = pl.BlockSpec(memory_space=pltpu.SMEM)
    return pl.pallas_call(
        partial(tiles_kernel, first),
        in_specs=[scalars, scalars, near] + [far] * 7,
        out_specs=[far] * 10 + [near],
        scratch_shapes=[
            pltpu.VMEM((8 * SPAN, K), jnp.bfloat16),
            pltpu.VMEM((8 * SPAN, K), jnp.bfloat16),
            pltpu.VMEM((16 * SPAN, K), jnp.bfloat16),
            pltpu.VMEM((4 * EXTRA, K), jnp.bfloat16),
            pltpu.VMEM((SLOTS, BLK, BLK), jnp.bfloat16),
            pltpu.VMEM((GROUP, BLK, BLK), jnp.bfloat16),
            pltpu.VMEM((8 * SPAN, K), jnp.float32),
            pltpu.VMEM((16 * SPAN, K), jnp.float32),
            pltpu.VMEM((8 * SPAN, K), jnp.bfloat16),
            pltpu.VMEM((8 * (SPAN + EXTRA), K), jnp.bfloat16),
            pltpu.VMEM((8 * (SPAN + EXTRA), K), jnp.bfloat16),
            pltpu.SemaphoreType.DMA((10,)),
            pltpu.SemaphoreType.DMA((SLOTS // GROUP,)),
            pltpu.SemaphoreType.DMA((10,)),
        ],
        out_shape=[jax.ShapeDtypeStruct((SPAN, K), jnp.bfloat16)] * 8
        + [
            jax.ShapeDtypeStruct((8 * (SPAN + EXTRA), K), jnp.bfloat16),
            jax.ShapeDtypeStruct((8 * (SPAN + EXTRA), K), jnp.bfloat16),
            jax.ShapeDtypeStruct((8, K), jnp.float32),
        ],
        compiler_params=pltpu.CompilerParams(vmem_limit_bytes=VMEM_MIB << 20),
        name="tiles",
    )(places, live, shares.reshape(1, K), *rows, own_in, other_in, tiles)


def after(value, *others):
    return lax.optimization_barrier((value, *others))[0]


def gather_words(weights, totals, tiles):
    copies = jnp.broadcast_to(weights[None], (8, SPAN, K))
    if totals is None:
        low = after(send(weights, "zl", 1), copies)
        row_sent = jnp.concatenate([weights, low])
    else:
        low = after(send(jnp.concatenate([weights, in_parts(totals)]), "zl", 1), copies)
        both = in_parts(totals + joined(low[SPAN:]))
        row_sent = jnp.concatenate([weights, low[:SPAN], both])
    rows = [row_sent] + [send(row_sent, "x", s) for s in (1, 2, 3)]
    copies = after(copies, row_sent)
    own = lax.all_to_all(copies, AXES, 0, 0, axis_index_groups=together("zh", "y"))
    if totals is None:
        tiles = after(tiles, row_sent).astype(jnp.bfloat16)
        own = after(own, tiles)
    own = after(own, *rows[1:])
    own = own.reshape(8 * SPAN, K)
    return (rows, own, send(own, "k", 1)), tiles


def scatter_terms(*outs):
    f32, b16 = jnp.float32, jnp.bfloat16
    x_outs, k_out, s_out = outs[:8], outs[8], outs[9]
    others = [send(x_outs[2 * s + 1], "x", s) for s in (1, 2, 3)]
    owns = [send(after(x_outs[2 * s], others[s - 1]), "x", s) for s in (1, 2, 3)]
    x_other = x_outs[1].astype(f32) + sum(x.astype(f32) for x in others)
    x_own = x_outs[0].astype(f32) + sum(x.astype(f32) for x in owns)
    s_got = send(s_out, "k", 1)
    sent = (k_out.astype(f32) + s_got.astype(f32)).astype(b16).reshape(8, SPAN + EXTRA, K)
    got = lax.all_to_all(sent, AXES, 0, 0, axis_index_groups=together("zh", "y"))
    low = send(x_other.astype(b16), "zl", 1)
    got = after(got, low, *owns)
    col_sum = jnp.sum(got[:, :SPAN].astype(f32), axis=0)
    totals = jnp.sum(got[:, SPAN:].astype(f32), axis=(0, 1))
    row_sum = x_own + low.astype(f32)
    return row_sum, col_sum, totals


def sum_columns(value, at):
    value = jnp.broadcast_to(value[None], (8, K))
    stack = jnp.stack([value] + [send(value, "x", s) for s in (3, 2, 1)])
    value = jnp.sum(jnp.roll(stack, at["x"], axis=0), axis=0)
    return (value + send(value, "zl", 1))[0]


def local(word_topic, topic_weight, tile_blocks, tile_live, pair_counts):
    at = coords()
    places = placed(tile_blocks[0, 0], at)
    live = tile_live.reshape(1)
    tiles = pair_counts.reshape(SLOTS, BLK, BLK)
    weights, shares, totals = word_topic, topic_weight, None
    for step in range(ITERS):
        gathered, tiles = gather_words(weights, totals, tiles)
        outs = sweep(step == 0, places, live, shares, *gathered, tiles)
        row_sum, col_sum, totals = scatter_terms(*outs[:-1])
        if step > 0:
            shares = outs[-1][0]
        expected = weights.astype(jnp.float32) * (shares * row_sum + col_sum)
        if step < ITERS - 1:
            weights = expected.astype(jnp.bfloat16)
    totals = sum_columns(totals, at)
    return (V * expected / totals).astype(jnp.bfloat16), K * totals / jnp.sum(totals)


def solution(mesh):
    in_specs = (
        P(("row", "col"), None),
        P(),
        P("row", "col", None, None),
        P("row", "col"),
        P("row", "col", None, None, None),
    )
    out_specs = (P(("row", "col"), None), P())
    return jax.shard_map(local, mesh=mesh, in_specs=in_specs, out_specs=out_specs, check_vma=False)
```
